1024 devices in a mesh: section: 16 (over z), dp: 32 (over y_lo, x, core), space: 2 (over y_hi).
Axes of the slice: x: 4, y: 8 (y_hi: 2, y_lo: 4; y = y_hi * 4 + y_lo), z: 16, core: 2. Of those that a mesh axis runs over, the one named last changes fastest.
Arguments:
- inputs: bfloat16 [16, 2, 32, 2, 8, 8, 256], P('section', None, 'dp', 'space'), may hold values from -6 to 6
- preacts: bfloat16 [16, 2, 32, 2, 8, 8, 256], P('section', None, 'dp', 'space'), may hold values from -6 to 6
- out_grad: bfloat16 [2, 32, 2, 8, 8, 256], P(None, 'dp', 'space'), may hold values from -6 to 6
- conv_w: bfloat16 [16, 27, 256, 256], P('section'), may hold values from -0.078125 to 0.078125
- proj_w: bfloat16 [16, 256, 256], P('section'), may hold values from -0.1875 to 0.1875
Outputs:
- section_grads: bfloat16 [16, 2, 32, 2, 8, 8, 256], P('section', None, 'dp', 'space')
- grad_conv: float32 [16, 256, 27, 256], P('section', 'dp')
- grad_proj: float32 [16, 256, 256], P('section', 'dp')
The draws below stay inside these ranges and needn't reach their ends.
All inputs are finite; a program needn't handle non-finite values.
Results may differ from the reference program's by a relative error of at most 0.029.
Values may be sent and summed in bfloat16 or wider, within the bound.
A program may use at most 32 MiB of HBM per device.

```python
import jax
import jax.numpy as jnp
from jax import lax

C = 256
HH = 8
WW = 8
DEP = 1
KK = 27
MICRO = 2
SECTIONS = 16
CROPS = 32
DEPTH = 2
N_SPACE = 2


def steps_of(stream_key, extent, cuts, smallest, largest):
    def one(position, shards_of):
        heights = jax.random.uniform(jax.random.fold_in(jax.random.fold_in(stream_key, 6), position), (shards_of,), jnp.float32, smallest / len(cuts), largest / len(cuts))
        return jnp.repeat(jnp.exp(heights), extent[position] // shards_of).reshape((-1,) + (1,) * (len(extent) - position - 1))

    factor_of = one(*cuts[0])
    for cut in cuts[1:]:
        factor_of = factor_of * one(*cut)
    return factor_of


def noise(stream_key, dims, width, most, split=(), held_as=jnp.bfloat16):
    values = jax.random.normal(stream_key, dims, jnp.float32) * width
    if len(split) > 0:
        values = steps_of(stream_key, dims, split, -0.22, 0.18) * values
    return jnp.clip(values, min=-most, max=most).astype(held_as)


def setup_inputs(seed: int = 0) -> dict:
    key_list = jax.random.split(jax.random.key(seed), 6)
    inputs = noise(key_list[0], (SECTIONS, MICRO, CROPS, DEPTH, HH, WW, C), 1.0, 6.0, ((0, 16), (2, 32), (3, 2)))
    preacts = noise(key_list[1], (SECTIONS, MICRO, CROPS, DEPTH, HH, WW, C), 1.0, 6.0, ((0, 16), (2, 32), (3, 2)))
    out_grad = noise(key_list[2], (MICRO, CROPS, DEPTH, HH, WW, C), 1.0, 6.0, ((1, 32), (2, 2)))
    conv_w = noise(key_list[3], (SECTIONS, KK, C, C), (KK * C) ** -0.5, 0.078125, ((0, 16),))
    proj_w = noise(key_list[4], (SECTIONS, C, C), (4 * C) ** -0.5, 0.1875, ((0, 16),))
    return {"inputs": inputs, "preacts": preacts, "out_grad": out_grad, "conv_w": conv_w, "proj_w": proj_w}


def tap_offsets():
    return [(depth_off, row_off, col_off) for depth_off in (-1, 0, 1) for row_off in (-1, 0, 1) for col_off in (-1, 0, 1)]


def slab_terms(left, right, scale_term):
    left_slabs = left.reshape(MICRO, CROPS, N_SPACE, DEP * HH * WW, C).astype(jnp.float32)
    right_slabs = right.reshape(MICRO, CROPS, N_SPACE, DEP * HH * WW, C).astype(jnp.float32)
    terms = jnp.einsum('mbprc,mbprd->bpcd', left_slabs, right_slabs) * scale_term
    rounded = lax.optimization_barrier(terms.astype(jnp.bfloat16)).astype(jnp.float32)
    return jnp.sum(rounded, axis=(0, 1))


def reference(inputs, preacts, out_grad, conv_w, proj_w):
    offsets = tap_offsets()
    scale_term = 1.0 / (MICRO * CROPS)
    widths = ((0, 0), (0, 0), (1, 1), (1, 1), (1, 1), (0, 0))
    incoming = out_grad
    section_list = [None] * SECTIONS
    conv_list = [None] * SECTIONS
    proj_list = [None] * SECTIONS
    for section in range(SECTIONS - 1, -1, -1):
        acts = inputs[section]
        pre_acts = preacts[section]
        hidden = jnp.maximum(pre_acts, jnp.zeros((), jnp.bfloat16))
        grad_hidden = jnp.einsum('mbzyxo,ho->mbzyxh', incoming.astype(jnp.float32), proj_w[section].astype(jnp.float32))
        grad_pre = jnp.where(pre_acts > 0, grad_hidden, jnp.zeros((), jnp.float32)).astype(jnp.bfloat16)
        padded_grad = jnp.pad(grad_pre, widths)
        padded_acts = jnp.pad(acts, widths)
        total = incoming.astype(jnp.float32)
        conv_rows = []
        for index, (depth_off, row_off, col_off) in enumerate(offsets):
            weight = conv_w[section, index].astype(jnp.float32)
            moved = padded_grad[:, :, 1 - depth_off:1 - depth_off + DEPTH, 1 - row_off:1 - row_off + HH, 1 - col_off:1 - col_off + WW]
            total = total + jnp.einsum('mbzyxo,io->mbzyxi', moved.astype(jnp.float32), weight)
            shifted = padded_acts[:, :, 1 + depth_off:1 + depth_off + DEPTH, 1 + row_off:1 + row_off + HH, 1 + col_off:1 + col_off + WW]
            conv_rows.append(slab_terms(shifted, grad_pre, scale_term))
        grad_in = total.astype(jnp.bfloat16)
        section_list[section] = grad_in
        conv_list[section] = jnp.stack(conv_rows, axis=1)
        proj_list[section] = slab_terms(hidden, incoming, scale_term)
        incoming = grad_in
    return jnp.stack(section_list), jnp.stack(conv_list), jnp.stack(proj_list)
```

```python
import functools

import jax
import jax.numpy as jnp
from jax import lax
from jax.experimental import pallas as pl
from jax.experimental.pallas import tpu as pltpu
from jax.sharding import PartitionSpec as P

MESH = pl.DeviceIdType.MESH
BF = jnp.bfloat16
F32 = jnp.float32
NX, NY, NLO = 4, 8, 4
CHUNKS = 7
ROWS = 32
NT = (((1,), (1,)), ((), ()))


def kernel(
    x_hbm, pre_hbm, og_hbm, cw_hbm, pw_hbm,
    sg_out, gc_out, gp_out,
    xb, preb, ogb, cw, pw, pre32, gb, gob, planes, sg_in, shifted, grads,
    left, left_last, t_other, t_own, core_in, s_buf, x_in1, x_out, x_in2, r_buf, y_in, f_buf, f_in,
    lsem, psend, precv, rsend, rrecv, osend, orecv, csend, crecv, xsend, xrecv, ysend, yrecv, fsend, frecv,
):
    s = lax.axis_index("section")
    dp = lax.axis_index("dp")
    p = lax.axis_index("space")
    last = lax.axis_size("section") - 1
    core = lax.rem(dp, 2)
    xx = lax.rem(lax.div(dp, 2), NX)
    ylo = lax.div(dp, 2 * NX)
    yy = p * NLO + ylo
    other = 1 - p
    scale = 1.0 / (2 * lax.axis_size("dp"))

    def at_dp(x, y_lo, c):
        return (y_lo * NX + x) * 2 + c

    x_right, x_left = lax.rem(xx + 1, NX), lax.rem(xx + NX - 1, NX)
    x_far = lax.rem(xx + 2, NX)
    partner = {"space": other}
    core_peer = {"dp": at_dp(xx, ylo, 1 - core)}
    right = {"dp": at_dp(x_right, ylo, core)}
    left_dev = {"dp": at_dp(x_left, ylo, core)}

    def y_dev(k):
        t = lax.rem(yy + k, NY)
        return t, {"dp": at_dp(xx, lax.rem(t, NLO), core), "space": lax.div(t, NLO)}

    local = [
        pltpu.make_async_copy(pre_hbm.at[p], preb.at[p], lsem.at[0]),
        pltpu.make_async_copy(og_hbm.at[p], ogb.at[p], lsem.at[1]),
        pltpu.make_async_copy(pw_hbm, pw, lsem.at[2]),
        pltpu.make_async_copy(cw_hbm, cw, lsem.at[3]),
        pltpu.make_async_copy(x_hbm.at[p], xb.at[p], lsem.at[4]),
    ]
    for copy in local:
        copy.start()

    barrier = pltpu.get_barrier_semaphore()

    def greet(device):
        pl.semaphore_signal(barrier, inc=1, device_id=device, device_id_type=MESH)

    count = last + 1
    greet({"section": lax.rem(s + 1, count)})
    greet({"section": lax.rem(s + last, count)})
    greet(core_peer)
    greet(right)
    greet(left_dev)
    for k in range(1, NY):
        greet(y_dev(k)[1])

    pl.semaphore_wait(barrier, 5 + NY - 1)

    def remote(src, dst, ssem, rsem, device):
        return pltpu.make_async_remote_copy(
            src_ref=src, dst_ref=dst, send_sem=ssem, recv_sem=rsem, device_id=device, device_id_type=MESH
        )

    swaps = [
        remote(pre_hbm.at[other], preb.at[p], psend.at[0], precv.at[0], partner),
        remote(og_hbm.at[other], ogb.at[p], psend.at[1], precv.at[1], partner),
        remote(x_hbm.at[other], xb.at[p], psend.at[2], precv.at[2], partner),
    ]
    for copy in swaps:
        copy.start()

    def both(ref):
        pair = jnp.stack([ref[0].astype(F32), ref[1].astype(F32)], axis=1)
        return pair.reshape(128, 256)

    edge = jnp.zeros((3, 3, 16, 256), BF)
    shifted[:, :, 0:16] = edge
    shifted[:, :, 144:160] = edge
    local[0].wait()
    swaps[0].wait()
    pre32[...] = both(preb)
    local[1].wait()
    swaps[1].wait()

    @pl.when(s == last)
    def _():
        gb[...] = both(ogb).astype(BF)

    local[2].wait()

    def lanes():
        v = lax.broadcasted_iota(jnp.int32, (256, 128), 1)
        return v // 16, (v // 8) % 2, v % 8

    def build_left():
        local[4].wait()
        swaps[2].wait()
        xt = both(xb).T
        hid = jnp.maximum(pre32[...], 0.0).T
        lh, ld, lw = lanes()
        slabs = []
        for kd in (-1, 0, 1):
            for kh in (-1, 0, 1):
                for kw in (-1, 0, 1):
                    slabs.append((kd, kh, kw))

        def slab(index):
            kd, kh, kw = slabs[index]
            off = 16 * kh + 8 * kd + kw
            moved = xt if off == 0 else pltpu.roll(xt, (-off) % 128, 1)
            good = None
            for pos, k, top in ((lh, kh, 7), (ld, kd, 1), (lw, kw, 7)):
                if k != 0:
                    ok = pos >= 1 if k < 0 else pos <= top - 1
                    good = ok if good is None else good & ok
            if good is not None:
                moved = jnp.where(good, moved, 0.0)
            return moved.reshape(16, 2, 8, 128)

        zero = jnp.zeros((16, 2, 8, 128), F32)
        for chunk in range(CHUNKS):
            for pair in range(2):
                first = chunk * 4 + pair * 2
                a = slab(first)
                b = slab(first + 1) if first + 1 < 27 else zero
                tile = jnp.concatenate([a, b], axis=2).astype(BF)
                for c in range(2):
                    if chunk < CHUNKS - 1:
                        left[chunk, c, :, 16 * pair : 16 * pair + 16, :] = tile[:, c]
                    else:
                        left_last[c, :, 16 * pair : 16 * pair + 16, 0:128] = tile[:, c]
        h4 = hid.reshape(16, 2, 8, 128)
        tail = jnp.concatenate([zero, h4], axis=2).astype(BF)
        none = jnp.zeros((16, 16, 128), BF)
        for c in range(2):
            left_last[c, :, 0:16, 128:256] = none
            left_last[c, :, 16:32, 128:256] = tail[:, c]

    def open_block():
        g = gb[...]
        gh = lax.dot_general(g, pw[...], NT, preferred_element_type=F32)
        gpb = jnp.where(pre32[...] > 0, gh, 0.0).astype(BF)
        grads[0:128, :] = gpb
        grads[128:256, :] = g
        return gpb

    def close_block():
        gq = grads[0:128, :].astype(F32).reshape(16, 8, 256)
        w = lax.broadcasted_iota(jnp.int32, (16, 8, 256), 1)
        zeros = jnp.zeros((8, 8, 256), F32)
        for kw in (-1, 0, 1):
            if kw == 0:
                sw = gq
            elif kw == 1:
                sw = jnp.where(w >= 1, pltpu.roll(gq, 1, 1), 0.0)
            else:
                sw = jnp.where(w <= 6, pltpu.roll(gq, 7, 1), 0.0)
            s4 = sw.reshape(8, 2, 8, 256)
            for kd in (-1, 0, 1):
                if kd == 0:
                    val = s4
                elif kd == 1:
                    val = jnp.stack([zeros, s4[:, 0]], axis=1)
                else:
                    val = jnp.stack([s4[:, 1], zeros], axis=1)
                shifted[kd + 1, kw + 1, 16:144, :] = val.reshape(128, 256).astype(BF)
        accs = [gb[...].astype(F32), None]
        index = 0
        for kd in (-1, 0, 1):
            for kh in (-1, 0, 1):
                for kw in (-1, 0, 1):
                    rows = shifted[kd + 1, kw + 1, (1 - kh) * 16 : (1 - kh) * 16 + 128, :]
                    term = lax.dot_general(rows, cw[index], NT, preferred_element_type=F32)
                    side = index % 2
                    accs[side] = term if accs[side] is None else accs[side] + term
                    index += 1
        gob[...] = (accs[0] + accs[1]).astype(BF)

    hand = remote(gob, gb, rsend.at[0], rrecv.at[0], {"section": s - 1})

    @pl.when(s < last)
    def _():
        build_left()
        remote(gob, gb, rsend.at[0], rrecv.at[0], {"section": s + 1}).wait_recv()

    open_block()
    local[3].wait()

    @pl.when(s > 0)
    def _():
        close_block()
        hand.start()

    @pl.when(s == last)
    def _():
        build_left()

    back = remote(planes.at[other], sg_in, osend.at[0], orecv.at[0], partner)

    def give_back():
        @pl.when(s == 0)
        def _():
            close_block()

        gin = gob[...].astype(F32).reshape(8, 2, 8, 256)
        planes[0] = gin[:, 0].astype(BF)
        planes[1] = gin[:, 1].astype(BF)
        back.start()

    def product(chunk, c):
        if chunk < CHUNKS - 1:
            lhs = left[chunk, c].reshape(16 * ROWS, 128)
            rhs = grads[0:128, :]
        else:
            lhs = left_last[c].reshape(16 * ROWS, 256)
            rhs = grads[...]
        outs = []
        for part in range(2):
            span = slice(8 * ROWS * part, 8 * ROWS * (part + 1))
            out = jnp.dot(lhs[span], rhs, preferred_element_type=F32) * scale
            outs.append(out.astype(BF).reshape(NLO // 2, NX, ROWS, 256))
        return jnp.concatenate(outs, axis=0)

    core_copies = []
    for chunk in range(CHUNKS):
        t_other[chunk] = product(chunk, 1 - core)
        copy = remote(t_other.at[chunk], core_in.at[chunk], csend.at[chunk], crecv.at[chunk], core_peer)
        copy.start()
        core_copies.append(copy)
        t_own[chunk] = product(chunk, core)

    copies = []
    x1, x2, yc, fc = {}, {}, {}, {}

    def stage1(chunk):
        core_copies[chunk].wait_recv()
        for x in range(NX):
            s_buf[chunk, x] = (
                t_own[chunk, :, x].astype(F32) + core_in[chunk, :, x].astype(F32)
            ).astype(BF)
        far = s_buf.at[chunk, x_far]
        x1[chunk] = [
            remote(far.at[0:2], x_in1.at[chunk, 0], xsend.at[chunk, 0], xrecv.at[chunk, 0], right),
            remote(far.at[2:4], x_in1.at[chunk, 1], xsend.at[chunk, 1], xrecv.at[chunk, 1], left_dev),
        ]
        for copy in x1[chunk]:
            copy.start()

    def stage2(chunk):
        for copy in x1[chunk]:
            copy.wait_recv()
        to_right = s_buf[chunk, x_right]
        to_left = s_buf[chunk, x_left]
        x_out[chunk, 0, 0:2] = (to_right[0:2].astype(F32) + x_in1[chunk, 0].astype(F32)).astype(BF)
        x_out[chunk, 0, 2:4] = to_right[2:4]
        x_out[chunk, 1, 0:2] = to_left[0:2]
        x_out[chunk, 1, 2:4] = (to_left[2:4].astype(F32) + x_in1[chunk, 1].astype(F32)).astype(BF)
        x2[chunk] = [
            remote(x_out.at[chunk, 0], x_in2.at[chunk, 0], xsend.at[chunk, 2], xrecv.at[chunk, 2], right),
            remote(x_out.at[chunk, 1], x_in2.at[chunk, 1], xsend.at[chunk, 3], xrecv.at[chunk, 3], left_dev),
        ]
        for copy in x2[chunk]:
            copy.start()

    def stage3(chunk):
        for copy in x2[chunk]:
            copy.wait_recv()
        r_buf[chunk] = (
            s_buf[chunk, xx].astype(F32) + x_in2[chunk, 0].astype(F32) + x_in2[chunk, 1].astype(F32)
        ).astype(BF).reshape(NLO, 2, ROWS // 2, 256)
        yc[chunk] = []
        for k in range(1, NY):
            t, device = y_dev(k)
            copy = remote(
                r_buf.at[chunk, lax.rem(t, NLO), lax.div(t, NLO)],
                y_in.at[chunk, k - 1], ysend.at[chunk, k - 1], yrecv.at[chunk, k - 1], device,
            )
            copy.start()
            yc[chunk].append(copy)

    def stage4(chunk):
        total = r_buf[chunk, ylo, p].astype(F32)
        for k in range(1, NY):
            yc[chunk][k - 1].wait_recv()
            total = total + y_in[chunk, k - 1].astype(F32)
        f_buf[chunk] = total.astype(BF)
        fc[chunk] = remote(f_buf.at[chunk], f_in.at[chunk], fsend.at[chunk], frecv.at[chunk], partner)
        fc[chunk].start()

    def stage5(chunk):
        fc[chunk].wait_recv()
        mine = f_buf[chunk].astype(F32).reshape(2, 8, 256)
        theirs = f_in[chunk].astype(F32).reshape(2, 8, 256)
        low = jnp.where(p == 0, mine, theirs)
        high = jnp.where(p == 0, theirs, mine)
        gc_out[4 * chunk : 4 * chunk + 2] = low
        if chunk < CHUNKS - 1:
            gc_out[4 * chunk + 2 : 4 * chunk + 4] = high
        else:
            gc_out[4 * chunk + 2] = high[0]
            gp_out[...] = high[1]

    for chunk in range(CHUNKS):
        stage1(chunk)
    give_back()
    lags = ((stage2, 0), (stage3, 1), (stage4, 3), (stage5, 5))
    for t in range(CHUNKS + 5):
        for stage, lag in lags:
            if 0 <= t - lag < CHUNKS:
                stage(t - lag)

    back.wait_recv()
    sg_out[pl.ds(p, 1)] = planes[pl.ds(p, 1)]
    sg_out[pl.ds(other, 1)] = sg_in[...][None]

    back.wait_send()

    @pl.when(s > 0)
    def _():
        hand.wait_send()

    for chunk in range(CHUNKS):
        core_copies[chunk].wait_send()
        for copy in x1[chunk] + x2[chunk] + yc[chunk]:
            copy.wait_send()
        fc[chunk].wait_send()


def emit(a_in, b_in, c_in, a_out, b_out, c_out):
    a_out[...] = a_in[...]
    b_out[...] = b_in[...]
    c_out[...] = c_in[...]


def shards(inputs, preacts, out_grad, conv_w, proj_w):
    plane = (8, 8, 256)
    args = (
        inputs.reshape((2,) + plane),
        preacts.reshape((2,) + plane),
        out_grad.reshape((2,) + plane),
        conv_w.reshape(27, 256, 256),
        proj_w.reshape(256, 256),
    )
    half = ROWS // 2
    dma = pltpu.SemaphoreType.DMA
    vm = pltpu.VMEM
    scratch = [
        vm((2,) + plane, BF),
        vm((2,) + plane, BF),
        vm((2,) + plane, BF),
        vm((27, 256, 256), BF),
        vm((256, 256), BF),
        vm((128, 256), F32),
        vm((128, 256), BF),
        vm((128, 256), BF),
        vm((2,) + plane, BF),
        vm(plane, BF),
        vm((3, 3, 160, 256), BF),
        vm((256, 256), BF),
        vm((CHUNKS - 1, 2, 16, ROWS, 128), BF),
        vm((2, 16, ROWS, 256), BF),
        vm((CHUNKS, NLO, NX, ROWS, 256), BF),
        vm((CHUNKS, NLO, NX, ROWS, 256), BF),
        vm((CHUNKS, NLO, NX, ROWS, 256), BF),
        vm((CHUNKS, NX, NLO, ROWS, 256), BF),
        vm((CHUNKS, 2, 2, ROWS, 256), BF),
        vm((CHUNKS, 2, NLO, ROWS, 256), BF),
        vm((CHUNKS, 2, NLO, ROWS, 256), BF),
        vm((CHUNKS, NLO, 2, half, 256), BF),
        vm((CHUNKS, NY - 1, half, 256), BF),
        vm((CHUNKS, half, 256), BF),
        vm((CHUNKS, half, 256), BF),
        dma((5,)),
        dma((3,)),
        dma((3,)),
        dma((1,)),
        dma((1,)),
        dma((1,)),
        dma((1,)),
        dma((CHUNKS,)),
        dma((CHUNKS,)),
        dma((CHUNKS, 4)),
        dma((CHUNKS, 4)),
        dma((CHUNKS, NY - 1)),
        dma((CHUNKS, NY - 1)),
        dma((CHUNKS,)),
        dma((CHUNKS,)),
    ]
    sg, gc, gp = pl.pallas_call(
        kernel,
        out_shape=(
            jax.ShapeDtypeStruct((2,) + plane, BF),
            jax.ShapeDtypeStruct((27, 8, 256), F32),
            jax.ShapeDtypeStruct((8, 256), F32),
        ),
        in_specs=[pl.BlockSpec(memory_space=pl.ANY)] * 5,
        out_specs=(pl.BlockSpec(memory_space=pltpu.VMEM),) * 3,
        scratch_shapes=scratch,
        compiler_params=pltpu.CompilerParams(
            collective_id=0, has_side_effects=True, vmem_limit_bytes=60 * 1024 * 1024
        ),
        name="relay",
    )(*args)
    sg, gc, gp = pl.pallas_call(
        emit,
        out_shape=tuple(jax.ShapeDtypeStruct(a.shape, a.dtype) for a in (sg, gc, gp)),
        name="emit",
    )(sg, gc, gp)
    return (
        sg.reshape(1, 2, 1, 1, 8, 8, 256),
        jnp.transpose(gc, (1, 0, 2))[None],
        gp[None],
    )


def solution(mesh):
    placed = (
        P("section", None, "dp", "space", None, None, None),
        P("section", None, "dp", "space", None, None, None),
        P(None, "dp", "space", None, None, None),
        P("section", None, None, None),
        P("section", None, None),
    )
    return jax.shard_map(
        shards,
        mesh=mesh,
        in_specs=placed,
        out_specs=(
            P("section", None, "dp", "space", None, None, None),
            P("section", "dp", None, None),
            P("section", "dp", None),
        ),
        check_vma=False,
    )
```

```python
import functools

import jax
import jax.numpy as jnp
from jax import lax
from jax.experimental import pallas as pl
from jax.experimental.pallas import tpu as pltpu
from jax.sharding import PartitionSpec as P

MESH = pl.DeviceIdType.MESH
BF = jnp.bfloat16
F32 = jnp.float32
NX, NY, NLO = 4, 8, 4
CHUNKS = 7
ROWS = 32
NT = (((1,), (1,)), ((), ()))


def kernel(
    x_hbm, pre_hbm, og_hbm, cw_hbm, pw_hbm,
    sg_out, gc_out, gp_out,
    xb, preb, ogb, cw, pw, pre32, gb, gob, planes, sg_in, shifted, grads, cwt,
    left, left_last, t_other, core_in, s_buf, x_in1, x_out, x_in2, r_buf, y_in, y_last, f_buf, f_in,
    lsem, psend, precv, rsend, rrecv, osend, orecv, csend, crecv, xsend, xrecv, ysend, yrecv, fsend, frecv,
):
    s = lax.axis_index("section")
    dp = lax.axis_index("dp")
    p = lax.axis_index("space")
    last = lax.axis_size("section") - 1
    core = lax.rem(dp, 2)
    xx = lax.rem(lax.div(dp, 2), NX)
    ylo = lax.div(dp, 2 * NX)
    yy = p * NLO + ylo
    other = 1 - p
    scale = 1.0 / (2 * lax.axis_size("dp"))

    def at_dp(x, y_lo, c):
        return (y_lo * NX + x) * 2 + c

    x_right, x_left = lax.rem(xx + 1, NX), lax.rem(xx + NX - 1, NX)
    x_far = lax.rem(xx + 2, NX)
    partner = {"space": other}
    odd = lax.rem(s, 2)
    twin = at_dp(xx, ylo, 1 - core)
    core_peer = {"dp": twin}
    corner = {"dp": twin, "space": other}
    right = {"dp": at_dp(x_right, ylo, core)}
    left_dev = {"dp": at_dp(x_left, ylo, core)}

    def y_dev(k):
        t = lax.rem(yy + k, NY)
        return t, {"dp": at_dp(xx, lax.rem(t, NLO), core), "space": lax.div(t, NLO)}

    def fetch(src, dst, sem):
        copy = pltpu.make_async_copy(src, dst, sem)
        copy.start()
        return copy

    weights = [fetch(pw_hbm, pw, lsem.at[2]), fetch(cw_hbm, cw, lsem.at[3])]

    barrier = pltpu.get_barrier_semaphore()

    def greet(device):
        pl.semaphore_signal(barrier, inc=1, device_id=device, device_id_type=MESH)

    count = last + 1
    greet({"section": lax.rem(s + 1, count), "dp": twin})
    greet({"section": lax.rem(s + last, count), "dp": twin})
    greet(core_peer)
    greet(corner)
    greet(right)
    greet(left_dev)
    for k in range(1, NY):
        greet(y_dev(k)[1])

    pl.semaphore_wait(barrier, 6 + NY - 1)

    def remote(src, dst, ssem, rsem, device):
        return pltpu.make_async_remote_copy(
            src_ref=src, dst_ref=dst, send_sem=ssem, recv_sem=rsem, device_id=device, device_id_type=MESH
        )

    sources = ((pre_hbm, preb), (og_hbm, ogb), (x_hbm, xb))

    def own_local(n):
        src, dst = sources[n]
        return pltpu.make_async_copy(src.at[p], dst.at[p], lsem.at[4 + n])

    def own_remote(n):
        src, dst = sources[n]
        return remote(src.at[p], dst.at[p], psend.at[3 + n], precv.at[3 + n], core_peer)

    def swap(n, device):
        src, dst = sources[n]
        return remote(src.at[other], dst.at[p], psend.at[n], precv.at[n], device)

    @pl.when(odd == 0)
    def _():
        for n in range(3):
            swap(n, partner).start()
            own_local(n).start()

    @pl.when(odd == 1)
    def _():
        for n in range(3):
            swap(n, corner).start()
            own_remote(n).start()

    def landed(n):
        swap(n, partner).wait_recv()

        @pl.when(odd == 0)
        def _():
            own_local(n).wait()

        @pl.when(odd == 1)
        def _():
            own_remote(n).wait_recv()

    def both(ref):
        pair = jnp.stack([ref[0].astype(F32), ref[1].astype(F32)], axis=1)
        return pair.reshape(128, 256)

    edge = jnp.zeros((3, 3, 16, 256), BF)
    shifted[:, :, 0:16] = edge
    shifted[:, :, 144:160] = edge
    landed(0)
    pre32[...] = both(preb)
    landed(1)

    @pl.when(s == last)
    def _():
        gb[...] = both(ogb).astype(BF)

    weights[0].wait()

    def lanes():
        v = lax.broadcasted_iota(jnp.int32, (256, 128), 1)
        return v // 16, (v // 8) % 2, v % 8

    def build_left():
        landed(2)
        xt = both(xb).T
        hid = jnp.maximum(pre32[...], 0.0).T
        lh, ld, lw = lanes()
        slabs = []
        for kd in (-1, 0, 1):
            for kh in (-1, 0, 1):
                for kw in (-1, 0, 1):
                    slabs.append((kd, kh, kw))

        def slab(index):
            kd, kh, kw = slabs[index]
            off = 16 * kh + 8 * kd + kw
            moved = xt if off == 0 else pltpu.roll(xt, (-off) % 128, 1)
            good = None
            for pos, k, top in ((lh, kh, 7), (ld, kd, 1), (lw, kw, 7)):
                if k != 0:
                    ok = pos >= 1 if k < 0 else pos <= top - 1
                    good = ok if good is None else good & ok
            if good is not None:
                moved = jnp.where(good, moved, 0.0)
            return moved.reshape(16, 2, 8, 128)

        zero = jnp.zeros((16, 2, 8, 128), F32)
        for chunk in range(CHUNKS):
            for pair in range(2):
                first = chunk * 4 + pair * 2
                a = slab(first)
                b = slab(first + 1) if first + 1 < 27 else zero
                tile = jnp.concatenate([a, b], axis=2).astype(BF)
                for c in range(2):
                    if chunk < CHUNKS - 1:
                        left[chunk, c, :, 16 * pair : 16 * pair + 16, :] = tile[:, c]
                    else:
                        left_last[c, :, 16 * pair : 16 * pair + 16, 0:128] = tile[:, c]
        h4 = hid.reshape(16, 2, 8, 128)
        tail = jnp.concatenate([zero, h4], axis=2).astype(BF)
        none = jnp.zeros((16, 16, 128), BF)
        for c in range(2):
            left_last[c, :, 0:16, 128:256] = none
            left_last[c, :, 16:32, 128:256] = tail[:, c]

    def open_block():
        g = gb[...]
        gh = lax.dot_general(g, pw[...], NT, preferred_element_type=F32)
        gpb = jnp.where(pre32[...] > 0, gh, 0.0).astype(BF)
        grads[0:128, :] = gpb
        grads[128:256, :] = g
        return gpb

    def turn_weights():
        @pl.loop(0, 27)
        def _(k):
            cwt[k] = cw[k].T

    def close_block(turned):
        gq = grads[0:128, :].astype(F32).reshape(16, 8, 256)
        w = lax.broadcasted_iota(jnp.int32, (16, 8, 256), 1)
        zeros = jnp.zeros((8, 8, 256), F32)
        for kw in (-1, 0, 1):
            if kw == 0:
                sw = gq
            elif kw == 1:
                sw = jnp.where(w >= 1, pltpu.roll(gq, 1, 1), 0.0)
            else:
                sw = jnp.where(w <= 6, pltpu.roll(gq, 7, 1), 0.0)
            s4 = sw.reshape(8, 2, 8, 256)
            for kd in (-1, 0, 1):
                if kd == 0:
                    val = s4
                elif kd == 1:
                    val = jnp.stack([zeros, s4[:, 0]], axis=1)
                else:
                    val = jnp.stack([s4[:, 1], zeros], axis=1)
                shifted[kd + 1, kw + 1, 16:144, :] = val.reshape(128, 256).astype(BF)
        accs = [gb[...].astype(F32), None]
        index = 0
        for kd in (-1, 0, 1):
            for kh in (-1, 0, 1):
                for kw in (-1, 0, 1):
                    rows = shifted[kd + 1, kw + 1, (1 - kh) * 16 : (1 - kh) * 16 + 128, :]
                    if turned:
                        term = jnp.dot(rows, cwt[index], preferred_element_type=F32)
                    else:
                        term = lax.dot_general(rows, cw[index], NT, preferred_element_type=F32)
                    side = index % 2
                    accs[side] = term if accs[side] is None else accs[side] + term
                    index += 1
        gob[...] = (accs[0] + accs[1]).astype(BF)

    hand = remote(gob, gb, rsend.at[0], rrecv.at[0], {"section": s - 1, "dp": twin})

    early = (s == last) & (core == 0)
    weights[1].wait()

    @pl.when(s < last)
    def _():
        turn_weights()

    @pl.when(jnp.logical_not(early))
    def _():
        build_left()

    @pl.when(s < last)
    def _():
        remote(gob, gb, rsend.at[0], rrecv.at[0], {"section": s + 1, "dp": twin}).wait_recv()

    open_block()

    @pl.when(s == last)
    def _():
        close_block(False)
        hand.start()

    @pl.when((s > 0) & (s < last))
    def _():
        close_block(True)
        hand.start()

    @pl.when(early)
    def _():
        build_left()

    def back(device):
        return remote(planes.at[other], sg_in.at[p], osend.at[0], orecv.at[0], device)

    def back_own():
        return remote(planes.at[p], sg_in.at[p], osend.at[1], orecv.at[1], core_peer)

    def give_back():
        @pl.when(s == 0)
        def _():
            close_block(True)

        gin = gob[...].astype(F32).reshape(8, 2, 8, 256)
        planes[0] = gin[:, 0].astype(BF)
        planes[1] = gin[:, 1].astype(BF)

        @pl.when(odd == 0)
        def _():
            back(partner).start()

        @pl.when(odd == 1)
        def _():
            back(corner).start()
            back_own().start()

    def product(chunk, c):
        if chunk < CHUNKS - 1:
            lhs = left[chunk, c].reshape(16 * ROWS, 128)
            rhs = grads[0:128, :]
        else:
            lhs = left_last[c].reshape(16 * ROWS, 256)
            rhs = grads[...]
        outs = []
        for part in range(2):
            span = slice(8 * ROWS * part, 8 * ROWS * (part + 1))
            out = jnp.dot(lhs[span], rhs, preferred_element_type=F32) * scale
            outs.append(out.reshape(NLO // 2, NX, ROWS, 256))
        return outs

    core_copies = []
    for chunk in range(CHUNKS):
        for part, out in enumerate(product(chunk, 1 - core)):
            t_other[chunk, 2 * part : 2 * part + 2] = out.astype(BF)
        copy = remote(t_other.at[chunk], core_in.at[chunk], csend.at[chunk], crecv.at[chunk], core_peer)
        copy.start()
        core_copies.append(copy)

    x1, x2, yc, fc = {}, {}, {}, {}

    def stage1(chunk):
        own = product(chunk, core)
        core_copies[chunk].wait_recv()
        for part in range(2):
            for x in range(NX):
                s_buf[chunk, x, 2 * part : 2 * part + 2] = (
                    own[part][:, x] + core_in[chunk, 2 * part : 2 * part + 2, x].astype(F32)
                ).astype(BF)
        far = s_buf.at[chunk, x_far]
        x1[chunk] = [
            remote(far.at[0:2], x_in1.at[chunk, 0], xsend.at[chunk, 0], xrecv.at[chunk, 0], right),
            remote(far.at[2:4], x_in1.at[chunk, 1], xsend.at[chunk, 1], xrecv.at[chunk, 1], left_dev),
        ]
        for copy in x1[chunk]:
            copy.start()

    def stage2(chunk):
        for copy in x1[chunk]:
            copy.wait_recv()
        to_right = s_buf[chunk, x_right]
        to_left = s_buf[chunk, x_left]
        x_out[chunk, 0, 0:2] = (to_right[0:2].astype(F32) + x_in1[chunk, 0].astype(F32)).astype(BF)
        x_out[chunk, 0, 2:4] = to_right[2:4]
        x_out[chunk, 1, 0:2] = to_left[0:2]
        x_out[chunk, 1, 2:4] = (to_left[2:4].astype(F32) + x_in1[chunk, 1].astype(F32)).astype(BF)
        x2[chunk] = [
            remote(x_out.at[chunk, 0], x_in2.at[chunk, 0], xsend.at[chunk, 2], xrecv.at[chunk, 2], right),
            remote(x_out.at[chunk, 1], x_in2.at[chunk, 1], xsend.at[chunk, 3], xrecv.at[chunk, 3], left_dev),
        ]
        for copy in x2[chunk]:
            copy.start()

    def stage3(chunk):
        for copy in x2[chunk]:
            copy.wait_recv()
        r_buf[chunk] = (
            s_buf[chunk, xx].astype(F32) + x_in2[chunk, 0].astype(F32) + x_in2[chunk, 1].astype(F32)
        ).astype(BF).reshape(NLO, 2, ROWS // 2, 256)
        yc[chunk] = []
        for k in range(1, NY):
            t, device = y_dev(k)
            if chunk == CHUNKS - 1:
                src, dst = r_buf.at[chunk, lax.rem(t, NLO)], y_last.at[yy]
            else:
                src, dst = r_buf.at[chunk, lax.rem(t, NLO), lax.div(t, NLO)], y_in.at[chunk, k - 1]
            copy = remote(
                src, dst, ysend.at[chunk, k - 1], yrecv.at[chunk, k - 1], device,
            )
            copy.start()
            yc[chunk].append(copy)

    def stage4(chunk):
        if chunk == CHUNKS - 1:
            y_last[pl.ds(yy, 1)] = r_buf[chunk, pl.ds(ylo, 1)]
            for copy in yc[chunk]:
                copy.wait_recv()
            total = y_last[0].astype(F32)
            for t in range(1, NY):
                total = total + y_last[t].astype(F32)
            total = total.reshape(4, 8, 256)
            gc_out[4 * chunk : 4 * chunk + 3] = total[0:3]
            gp_out[...] = total[3]
            return
        total = r_buf[chunk, ylo, p].astype(F32)
        for k in range(1, NY):
            yc[chunk][k - 1].wait_recv()
            total = total + y_in[chunk, k - 1].astype(F32)
        f_buf[chunk] = total.astype(BF)
        fc[chunk] = remote(f_buf.at[chunk], f_in.at[chunk], fsend.at[chunk], frecv.at[chunk], partner)
        fc[chunk].start()

    def stage5(chunk):
        fc[chunk].wait_recv()
        mine = f_buf[chunk].astype(F32).reshape(2, 8, 256)
        theirs = f_in[chunk].astype(F32).reshape(2, 8, 256)
        low = jnp.where(p == 0, mine, theirs)
        high = jnp.where(p == 0, theirs, mine)
        gc_out[4 * chunk : 4 * chunk + 2] = low
        gc_out[4 * chunk + 2 : 4 * chunk + 4] = high

    for chunk in range(CHUNKS):
        stage1(chunk)
    give_back()
    lags = ((stage2, 0), (stage3, 1), (stage4, 3), (stage5, 5))
    for t in range(CHUNKS + 5):
        for stage, lag in lags:
            if 0 <= t - lag < CHUNKS - (lag == 5):
                stage(t - lag)

    back(partner).wait_recv()
    sg_out[pl.ds(other, 1)] = sg_in[pl.ds(other, 1)]

    @pl.when(odd == 0)
    def _():
        sg_out[pl.ds(p, 1)] = planes[pl.ds(p, 1)]

    @pl.when(odd == 1)
    def _():
        back_own().wait_recv()
        sg_out[pl.ds(p, 1)] = sg_in[pl.ds(p, 1)]
        back_own().wait_send()
        for n in range(3):
            own_remote(n).wait_send()

    back(partner).wait_send()
    for n in range(3):
        swap(n, partner).wait_send()

    @pl.when(s > 0)
    def _():
        hand.wait_send()

    for chunk in range(CHUNKS):
        core_copies[chunk].wait_send()
        for copy in x1[chunk] + x2[chunk] + yc[chunk]:
            copy.wait_send()
        if chunk in fc:
            fc[chunk].wait_send()


def emit(a_in, b_in, c_in, a_out, b_out, c_out):
    a_out[...] = a_in[...]
    b_out[...] = b_in[...]
    c_out[...] = c_in[...]


def shards(inputs, preacts, out_grad, conv_w, proj_w):
    plane = (8, 8, 256)
    args = (
        inputs.reshape((2,) + plane),
        preacts.reshape((2,) + plane),
        out_grad.reshape((2,) + plane),
        conv_w.reshape(27, 256, 256),
        proj_w.reshape(256, 256),
    )
    half = ROWS // 2
    dma = pltpu.SemaphoreType.DMA
    vm = pltpu.VMEM
    scratch = [
        vm((2,) + plane, BF),
        vm((2,) + plane, BF),
        vm((2,) + plane, BF),
        vm((27, 256, 256), BF),
        vm((256, 256), BF),
        vm((128, 256), F32),
        vm((128, 256), BF),
        vm((128, 256), BF),
        vm((2,) + plane, BF),
        vm((2,) + plane, BF),
        vm((3, 3, 160, 256), BF),
        vm((256, 256), BF),
        vm((27, 256, 256), BF),
        vm((CHUNKS - 1, 2, 16, ROWS, 128), BF),
        vm((2, 16, ROWS, 256), BF),
        vm((CHUNKS, NLO, NX, ROWS, 256), BF),
        vm((CHUNKS, NLO, NX, ROWS, 256), BF),
        vm((CHUNKS, NX, NLO, ROWS, 256), BF),
        vm((CHUNKS, 2, 2, ROWS, 256), BF),
        vm((CHUNKS, 2, NLO, ROWS, 256), BF),
        vm((CHUNKS, 2, NLO, ROWS, 256), BF),
        vm((CHUNKS, NLO, 2, half, 256), BF),
        vm((CHUNKS, NY - 1, half, 256), BF),
        vm((NY, 2, half, 256), BF),
        vm((CHUNKS, half, 256), BF),
        vm((CHUNKS, half, 256), BF),
        dma((7,)),
        dma((6,)),
        dma((6,)),
        dma((1,)),
        dma((1,)),
        dma((2,)),
        dma((2,)),
        dma((CHUNKS,)),
        dma((CHUNKS,)),
        dma((CHUNKS, 4)),
        dma((CHUNKS, 4)),
        dma((CHUNKS, NY - 1)),
        dma((CHUNKS, NY - 1)),
        dma((CHUNKS,)),
        dma((CHUNKS,)),
    ]
    sg, gc, gp = pl.pallas_call(
        kernel,
        out_shape=(
            jax.ShapeDtypeStruct((2,) + plane, BF),
            jax.ShapeDtypeStruct((27, 8, 256), F32),
            jax.ShapeDtypeStruct((8, 256), F32),
        ),
        in_specs=[pl.BlockSpec(memory_space=pl.ANY)] * 5,
        out_specs=(pl.BlockSpec(memory_space=pltpu.VMEM),) * 3,
        scratch_shapes=scratch,
        compiler_params=pltpu.CompilerParams(
            collective_id=0, has_side_effects=True, vmem_limit_bytes=60 * 1024 * 1024
        ),
        name="relay",
    )(*args)
    sg, gc, gp = pl.pallas_call(
        emit,
        out_shape=tuple(jax.ShapeDtypeStruct(a.shape, a.dtype) for a in (sg, gc, gp)),
        name="emit",
    )(sg, gc, gp)
    return (
        sg.reshape(1, 2, 1, 1, 8, 8, 256),
        jnp.transpose(gc, (1, 0, 2))[None],
        gp[None],
    )


def solution(mesh):
    placed = (
        P("section", None, "dp", "space", None, None, None),
        P("section", None, "dp", "space", None, None, None),
        P(None, "dp", "space", None, None, None),
        P("section", None, None, None),
        P("section", None, None),
    )
    return jax.shard_map(
        shards,
        mesh=mesh,
        in_specs=placed,
        out_specs=(
            P("section", None, "dp", "space", None, None, None),
            P("section", "dp", None, None),
            P("section", "dp", None),
        ),
        check_vma=False,
    )
```

```python
import functools

import jax
import jax.numpy as jnp
from jax import lax
from jax.experimental import pallas as pl
from jax.experimental.pallas import tpu as pltpu
from jax.sharding import PartitionSpec as P

MESH = pl.DeviceIdType.MESH
BF = jnp.bfloat16
F32 = jnp.float32
NX, NY, NLO = 4, 8, 4
CHUNKS = 7
ROWS = 32
NT = (((1,), (1,)), ((), ()))


def kernel(
    x_hbm, pre_hbm, og_hbm, cw_hbm, pw_hbm,
    sg_out, gc_out, gp_out,
    xb, preb, ogb, cw, pw, pre32, gb, gob, planes, sg_in, shifted, grads, cwt,
    left, left_last, t_other, core_in, s_buf, x_in1, x_out, x_in2, r_buf, y_in, y_last, f_buf, f_in,
    lsem, psend, precv, rsend, rrecv, osend, orecv, csend, crecv, xsend, xrecv, ysend, yrecv, fsend, frecv,
):
    s = lax.axis_index("section")
    dp = lax.axis_index("dp")
    p = lax.axis_index("space")
    last = lax.axis_size("section") - 1
    core = lax.rem(dp, 2)
    xx = lax.rem(lax.div(dp, 2), NX)
    ylo = lax.div(dp, 2 * NX)
    yy = p * NLO + ylo
    other = 1 - p
    scale = 1.0 / (2 * lax.axis_size("dp"))

    def at_dp(x, y_lo, c):
        return (y_lo * NX + x) * 2 + c

    x_right, x_left = lax.rem(xx + 1, NX), lax.rem(xx + NX - 1, NX)
    x_far = lax.rem(xx + 2, NX)
    partner = {"space": other}
    odd = lax.rem(s, 2)
    twin = at_dp(xx, ylo, 1 - core)
    core_peer = {"dp": twin}
    corner = {"dp": twin, "space": other}
    right = {"dp": at_dp(x_right, ylo, core)}
    left_dev = {"dp": at_dp(x_left, ylo, core)}

    def y_dev(k):
        t = lax.rem(yy + k, NY)
        return t, {"dp": at_dp(xx, lax.rem(t, NLO), core), "space": lax.div(t, NLO)}

    def fetch(src, dst, sem):
        copy = pltpu.make_async_copy(src, dst, sem)
        copy.start()
        return copy

    weights = [fetch(pw_hbm, pw, lsem.at[2]), fetch(cw_hbm, cw, lsem.at[3])]

    barrier = pltpu.get_barrier_semaphore()

    def greet(device):
        pl.semaphore_signal(barrier, inc=1, device_id=device, device_id_type=MESH)

    count = last + 1
    greet({"section": lax.rem(s + 1, count), "dp": twin})
    greet({"section": lax.rem(s + last, count), "dp": twin})
    greet(core_peer)
    greet(corner)
    greet(right)
    greet(left_dev)
    for k in range(1, NY):
        greet(y_dev(k)[1])

    pl.semaphore_wait(barrier, 6 + NY - 1)

    def remote(src, dst, ssem, rsem, device):
        return pltpu.make_async_remote_copy(
            src_ref=src, dst_ref=dst, send_sem=ssem, recv_sem=rsem, device_id=device, device_id_type=MESH
        )

    sources = ((pre_hbm, preb), (og_hbm, ogb), (x_hbm, xb))

    def own_local(n):
        src, dst = sources[n]
        return pltpu.make_async_copy(src.at[p], dst.at[p], lsem.at[4 + n])

    def own_remote(n):
        src, dst = sources[n]
        return remote(src.at[p], dst.at[p], psend.at[3 + n], precv.at[3 + n], core_peer)

    def swap(n, device):
        src, dst = sources[n]
        return remote(src.at[other], dst.at[p], psend.at[n], precv.at[n], device)

    @pl.when(odd == 0)
    def _():
        for n in range(3):
            swap(n, partner).start()
            own_local(n).start()

    @pl.when(odd == 1)
    def _():
        for n in range(3):
            swap(n, corner).start()
            own_remote(n).start()

    def landed(n):
        swap(n, partner).wait_recv()

        @pl.when(odd == 0)
        def _():
            own_local(n).wait()

        @pl.when(odd == 1)
        def _():
            own_remote(n).wait_recv()

    def both(ref):
        pair = jnp.stack([ref[0].astype(F32), ref[1].astype(F32)], axis=1)
        return pair.reshape(128, 256)

    edge = jnp.zeros((3, 3, 16, 256), BF)
    shifted[:, :, 0:16] = edge
    shifted[:, :, 144:160] = edge
    landed(0)
    pre32[...] = both(preb)
    landed(1)

    @pl.when(s == last)
    def _():
        gb[...] = both(ogb).astype(BF)

    weights[0].wait()

    def lanes():
        v = lax.broadcasted_iota(jnp.int32, (256, 128), 1)
        return v // 16, (v // 8) % 2, v % 8

    def build_left():
        landed(2)
        xt = both(xb).T
        hid = jnp.maximum(pre32[...], 0.0).T
        lh, ld, lw = lanes()
        slabs = []
        for kd in (-1, 0, 1):
            for kh in (-1, 0, 1):
                for kw in (-1, 0, 1):
                    slabs.append((kd, kh, kw))

        def slab(index):
            kd, kh, kw = slabs[index]
            off = 16 * kh + 8 * kd + kw
            moved = xt if off == 0 else pltpu.roll(xt, (-off) % 128, 1)
            good = None
            for pos, k, top in ((lh, kh, 7), (ld, kd, 1), (lw, kw, 7)):
                if k != 0:
                    ok = pos >= 1 if k < 0 else pos <= top - 1
                    good = ok if good is None else good & ok
            if good is not None:
                moved = jnp.where(good, moved, 0.0)
            return moved.reshape(16, 2, 8, 128)

        zero = jnp.zeros((16, 2, 8, 128), F32)
        for chunk in range(CHUNKS):
            for pair in range(2):
                first = chunk * 4 + pair * 2
                a = slab(first)
                b = slab(first + 1) if first + 1 < 27 else zero
                tile = jnp.concatenate([a, b], axis=2).astype(BF)
                for c in range(2):
                    if chunk < CHUNKS - 1:
                        left[chunk, c, :, 16 * pair : 16 * pair + 16, :] = tile[:, c]
                    else:
                        left_last[c, :, 16 * pair : 16 * pair + 16, 0:128] = tile[:, c]
        h4 = hid.reshape(16, 2, 8, 128)
        tail = jnp.concatenate([zero, h4], axis=2).astype(BF)
        none = jnp.zeros((16, 16, 128), BF)
        for c in range(2):
            left_last[c, :, 0:16, 128:256] = none
            left_last[c, :, 16:32, 128:256] = tail[:, c]

    def open_block():
        g = gb[...]
        gh = lax.dot_general(g, pw[...], NT, preferred_element_type=F32)
        gpb = jnp.where(pre32[...] > 0, gh, 0.0).astype(BF)
        grads[0:128, :] = gpb
        grads[128:256, :] = g
        return gpb

    def turn_weights():
        @pl.loop(0, 27)
        def _(k):
            cwt[k] = cw[k].T

    def close_block(turned):
        gq = grads[0:128, :].astype(F32).reshape(16, 8, 256)
        w = lax.broadcasted_iota(jnp.int32, (16, 8, 256), 1)
        zeros = jnp.zeros((8, 8, 256), F32)
        for kw in (-1, 0, 1):
            if kw == 0:
                sw = gq
            elif kw == 1:
                sw = jnp.where(w >= 1, pltpu.roll(gq, 1, 1), 0.0)
            else:
                sw = jnp.where(w <= 6, pltpu.roll(gq, 7, 1), 0.0)
            s4 = sw.reshape(8, 2, 8, 256)
            for kd in (-1, 0, 1):
                if kd == 0:
                    val = s4
                elif kd == 1:
                    val = jnp.stack([zeros, s4[:, 0]], axis=1)
                else:
                    val = jnp.stack([s4[:, 1], zeros], axis=1)
                shifted[kd + 1, kw + 1, 16:144, :] = val.reshape(128, 256).astype(BF)
        accs = [gb[...].astype(F32), None]
        index = 0
        for kd in (-1, 0, 1):
            for kh in (-1, 0, 1):
                for kw in (-1, 0, 1):
                    rows = shifted[kd + 1, kw + 1, (1 - kh) * 16 : (1 - kh) * 16 + 128, :]
                    if turned:
                        term = jnp.dot(rows, cwt[index], preferred_element_type=F32)
                    else:
                        term = lax.dot_general(rows, cw[index], NT, preferred_element_type=F32)
                    side = index % 2
                    accs[side] = term if accs[side] is None else accs[side] + term
                    index += 1
        gob[...] = (accs[0] + accs[1]).astype(BF)

    hand = remote(gob, gb, rsend.at[0], rrecv.at[0], {"section": s - 1, "dp": twin})

    early = (s == last) & (core == 0)
    weights[1].wait()

    @pl.when(s < last)
    def _():
        turn_weights()

    @pl.when(jnp.logical_not(early))
    def _():
        build_left()

    @pl.when(s < last)
    def _():
        remote(gob, gb, rsend.at[0], rrecv.at[0], {"section": s + 1, "dp": twin}).wait_recv()

    open_block()

    @pl.when(s == last)
    def _():
        close_block(False)
        hand.start()

    @pl.when((s > 0) & (s < last))
    def _():
        close_block(True)
        hand.start()

    @pl.when(early)
    def _():
        build_left()

    def back(device):
        return remote(planes.at[other], sg_in.at[p], osend.at[0], orecv.at[0], device)

    def back_own():
        return remote(planes.at[p], sg_in.at[p], osend.at[1], orecv.at[1], core_peer)

    def give_back():
        @pl.when(s == 0)
        def _():
            close_block(True)

        gin = gob[...].astype(F32).reshape(8, 2, 8, 256)
        planes[0] = gin[:, 0].astype(BF)
        planes[1] = gin[:, 1].astype(BF)

        @pl.when(odd == 0)
        def _():
            back(partner).start()

        @pl.when(odd == 1)
        def _():
            back(corner).start()
            back_own().start()

    def product(chunk, c):
        if chunk < CHUNKS - 1:
            lhs = left[chunk, c].reshape(16 * ROWS, 128)
            rhs = grads[0:128, :]
        else:
            lhs = left_last[c].reshape(16 * ROWS, 256)
            rhs = grads[...]
        outs = []
        for part in range(2):
            span = slice(8 * ROWS * part, 8 * ROWS * (part + 1))
            out = jnp.dot(lhs[span], rhs, preferred_element_type=F32) * scale
            outs.append(out.reshape(NLO // 2, NX, ROWS, 256))
        return outs

    core_copies = []
    for chunk in range(CHUNKS):
        for part, out in enumerate(product(chunk, 1 - core)):
            t_other[chunk, 2 * part : 2 * part + 2] = out.astype(BF)
        copy = remote(t_other.at[chunk], core_in.at[chunk], csend.at[chunk], crecv.at[chunk], core_peer)
        copy.start()
        core_copies.append(copy)

    x1, x2, yc, fc = {}, {}, {}, {}

    def stage1(chunk):
        own = product(chunk, core)
        core_copies[chunk].wait_recv()
        for part in range(2):
            for x in range(NX):
                s_buf[chunk, x, 2 * part : 2 * part + 2] = (
                    own[part][:, x] + core_in[chunk, 2 * part : 2 * part + 2, x].astype(F32)
                ).astype(BF)
        far = s_buf.at[chunk, x_far]
        x1[chunk] = [
            remote(far.at[0:2], x_in1.at[chunk, 0], xsend.at[chunk, 0], xrecv.at[chunk, 0], right),
            remote(far.at[2:4], x_in1.at[chunk, 1], xsend.at[chunk, 1], xrecv.at[chunk, 1], left_dev),
        ]
        for copy in x1[chunk]:
            copy.start()

    def stage2(chunk):
        for copy in x1[chunk]:
            copy.wait_recv()
        to_right = s_buf[chunk, x_right]
        to_left = s_buf[chunk, x_left]
        x_out[chunk, 0, 0:2] = (to_right[0:2].astype(F32) + x_in1[chunk, 0].astype(F32)).astype(BF)
        x_out[chunk, 0, 2:4] = to_right[2:4]
        x_out[chunk, 1, 0:2] = to_left[0:2]
        x_out[chunk, 1, 2:4] = (to_left[2:4].astype(F32) + x_in1[chunk, 1].astype(F32)).astype(BF)
        x2[chunk] = [
            remote(x_out.at[chunk, 0], x_in2.at[chunk, 0], xsend.at[chunk, 2], xrecv.at[chunk, 2], right),
            remote(x_out.at[chunk, 1], x_in2.at[chunk, 1], xsend.at[chunk, 3], xrecv.at[chunk, 3], left_dev),
        ]
        for copy in x2[chunk]:
            copy.start()

    def stage3(chunk):
        for copy in x2[chunk]:
            copy.wait_recv()
        r_buf[chunk] = (
            s_buf[chunk, xx].astype(F32) + x_in2[chunk, 0].astype(F32) + x_in2[chunk, 1].astype(F32)
        ).astype(BF).reshape(NLO, 2, ROWS // 2, 256)
        yc[chunk] = {}
        for k in (4, 3, 5, 2, 6, 1, 7):
            t, device = y_dev(k)
            if chunk == CHUNKS - 1:
                src, dst = r_buf.at[chunk, lax.rem(t, NLO)], y_last.at[yy]
            else:
                src, dst = r_buf.at[chunk, lax.rem(t, NLO), lax.div(t, NLO)], y_in.at[chunk, k - 1]
            copy = remote(
                src, dst, ysend.at[chunk, k - 1], yrecv.at[chunk, k - 1], device,
            )
            copy.start()
            yc[chunk][k] = copy

    def stage4(chunk):
        if chunk == CHUNKS - 1:
            y_last[pl.ds(yy, 1)] = r_buf[chunk, pl.ds(ylo, 1)]
            for k in range(1, NY):
                yc[chunk][k].wait_recv()
            total = y_last[0].astype(F32)
            for t in range(1, NY):
                total = total + y_last[t].astype(F32)
            total = total.reshape(4, 8, 256)
            gc_out[4 * chunk : 4 * chunk + 3] = total[0:3]
            gp_out[...] = total[3]
            return
        total = r_buf[chunk, ylo, p].astype(F32)
        for k in range(1, NY):
            yc[chunk][k].wait_recv()
            total = total + y_in[chunk, k - 1].astype(F32)
        f_buf[chunk] = total.astype(BF)
        fc[chunk] = remote(f_buf.at[chunk], f_in.at[chunk], fsend.at[chunk], frecv.at[chunk], partner)
        fc[chunk].start()

    def stage5(chunk):
        fc[chunk].wait_recv()
        mine = f_buf[chunk].astype(F32).reshape(2, 8, 256)
        theirs = f_in[chunk].astype(F32).reshape(2, 8, 256)
        low = jnp.where(p == 0, mine, theirs)
        high = jnp.where(p == 0, theirs, mine)
        gc_out[4 * chunk : 4 * chunk + 2] = low
        gc_out[4 * chunk + 2 : 4 * chunk + 4] = high

    lags = ((stage1, 0), (stage2, 2), (stage3, 4), (stage4, 6), (stage5, 8))
    for t in range(CHUNKS + 8):
        if t == 2:
            give_back()
        for stage, lag in lags:
            if 0 <= t - lag < CHUNKS - (lag == 8):
                stage(t - lag)

    back(partner).wait_recv()
    sg_out[pl.ds(other, 1)] = sg_in[pl.ds(other, 1)]

    @pl.when(odd == 0)
    def _():
        sg_out[pl.ds(p, 1)] = planes[pl.ds(p, 1)]

    @pl.when(odd == 1)
    def _():
        back_own().wait_recv()
        sg_out[pl.ds(p, 1)] = sg_in[pl.ds(p, 1)]
        back_own().wait_send()
        for n in range(3):
            own_remote(n).wait_send()

    back(partner).wait_send()
    for n in range(3):
        swap(n, partner).wait_send()

    @pl.when(s > 0)
    def _():
        hand.wait_send()

    for chunk in range(CHUNKS):
        core_copies[chunk].wait_send()
        for copy in x1[chunk] + x2[chunk] + [yc[chunk][k] for k in range(1, NY)]:
            copy.wait_send()
        if chunk in fc:
            fc[chunk].wait_send()


def emit(a_in, b_in, c_in, a_out, b_out, c_out):
    a_out[...] = a_in[...]
    b_out[...] = b_in[...]
    c_out[...] = c_in[...]


def shards(inputs, preacts, out_grad, conv_w, proj_w):
    plane = (8, 8, 256)
    args = (
        inputs.reshape((2,) + plane),
        preacts.reshape((2,) + plane),
        out_grad.reshape((2,) + plane),
        conv_w.reshape(27, 256, 256),
        proj_w.reshape(256, 256),
    )
    half = ROWS // 2
    dma = pltpu.SemaphoreType.DMA
    vm = pltpu.VMEM
    scratch = [
        vm((2,) + plane, BF),
        vm((2,) + plane, BF),
        vm((2,) + plane, BF),
        vm((27, 256, 256), BF),
        vm((256, 256), BF),
        vm((128, 256), F32),
        vm((128, 256), BF),
        vm((128, 256), BF),
        vm((2,) + plane, BF),
        vm((2,) + plane, BF),
        vm((3, 3, 160, 256), BF),
        vm((256, 256), BF),
        vm((27, 256, 256), BF),
        vm((CHUNKS - 1, 2, 16, ROWS, 128), BF),
        vm((2, 16, ROWS, 256), BF),
        vm((CHUNKS, NLO, NX, ROWS, 256), BF),
        vm((CHUNKS, NLO, NX, ROWS, 256), BF),
        vm((CHUNKS, NX, NLO, ROWS, 256), BF),
        vm((CHUNKS, 2, 2, ROWS, 256), BF),
        vm((CHUNKS, 2, NLO, ROWS, 256), BF),
        vm((CHUNKS, 2, NLO, ROWS, 256), BF),
        vm((CHUNKS, NLO, 2, half, 256), BF),
        vm((CHUNKS, NY - 1, half, 256), BF),
        vm((NY, 2, half, 256), BF),
        vm((CHUNKS, half, 256), BF),
        vm((CHUNKS, half, 256), BF),
        dma((7,)),
        dma((6,)),
        dma((6,)),
        dma((1,)),
        dma((1,)),
        dma((2,)),
        dma((2,)),
        dma((CHUNKS,)),
        dma((CHUNKS,)),
        dma((CHUNKS, 4)),
        dma((CHUNKS, 4)),
        dma((CHUNKS, NY - 1)),
        dma((CHUNKS, NY - 1)),
        dma((CHUNKS,)),
        dma((CHUNKS,)),
    ]
    sg, gc, gp = pl.pallas_call(
        kernel,
        out_shape=(
            jax.ShapeDtypeStruct((2,) + plane, BF),
            jax.ShapeDtypeStruct((27, 8, 256), F32),
            jax.ShapeDtypeStruct((8, 256), F32),
        ),
        in_specs=[pl.BlockSpec(memory_space=pl.ANY)] * 5,
        out_specs=(pl.BlockSpec(memory_space=pltpu.VMEM),) * 3,
        scratch_shapes=scratch,
        compiler_params=pltpu.CompilerParams(
            collective_id=0, has_side_effects=True, vmem_limit_bytes=60 * 1024 * 1024
        ),
        name="relay",
    )(*args)
    sg, gc, gp = pl.pallas_call(
        emit,
        out_shape=tuple(jax.ShapeDtypeStruct(a.shape, a.dtype) for a in (sg, gc, gp)),
        name="emit",
    )(sg, gc, gp)
    return (
        sg.reshape(1, 2, 1, 1, 8, 8, 256),
        jnp.transpose(gc, (1, 0, 2))[None],
        gp[None],
    )


def solution(mesh):
    placed = (
        P("section", None, "dp", "space", None, None, None),
        P("section", None, "dp", "space", None, None, None),
        P(None, "dp", "space", None, None, None),
        P("section", None, None, None),
        P("section", None, None),
    )
    return jax.shard_map(
        shards,
        mesh=mesh,
        in_specs=placed,
        out_specs=(
            P("section", None, "dp", "space", None, None, None),
            P("section", "dp", None, None),
            P("section", "dp", None),
        ),
        check_vma=False,
    )
```
